32 devices in a mesh: rad: 4 (over z), ma: 8 (over y, x, core).
Axes of the slice: x: 2, y: 2, z: 4, core: 2. Of those that a mesh axis runs over, the one named last changes fastest.
Arguments:
- spectrum: bfloat16 [4, 512, 512, 384], P(None, 'ma', 'rad'), may hold values from -6 to 6
- radial_table: bfloat16 [12, 384], replicated, may hold values from -0.3125 to 0.3125
- legendre: bfloat16 [512, 512, 512], P('ma', 'rad'), may hold values from -0.375 to 0.375
- order_table: int32 [512], replicated, may hold values from 0 to 511, each once
- cylinder_row: int32 [512, 12], P(('rad', 'ma')), may hold values from 0 to 127
- column_weight: float32 [512, 12], P(('rad', 'ma')), may hold values from 0.5 to 2
Outputs:
- column_buoyancy: float32 [128, 1024], P('ma', 'rad')
- advected: float32 [2, 512, 12, 1024], P(None, ('rad', 'ma'))
The draws below stay inside these ranges and needn't reach their ends.
Inputs may be any that keep to these rules, and one draw needn't show every extreme that they name: `order_table`: each order appears in exactly one slot.
All inputs are finite; a program needn't handle non-finite values.
Results may differ from the reference program's by a relative error of at most 0.008.
Values may be sent and summed in bfloat16 or wider, within the bound.
A program may use at most 128 MiB of HBM per device.

```python
import math
import jax
import jax.numpy as jnp
from jax import lax

L = 512
NCHEB = 384
NTH = 512
NPHI = 1024
NRAD = 12
NS = 128


def with_ends(drawn, stream_key, least, largest):
    longest = drawn.shape.index(max(drawn.shape))
    spots = []
    for shift in (0, 1):
        where = [jax.random.randint(jax.random.fold_in(stream_key, axis), (), 0, length) for axis, length in enumerate(drawn.shape)]
        where[longest] = (where[longest] + shift) % drawn.shape[longest]
        spots.append(tuple(where))
    return drawn.at[spots[0]].set(least).at[spots[1]].set(largest)


def shard_levels(key, dims, cuts, smallest, high):
    factor_of = 1.0
    for dim, parts in cuts:
        steps = jax.random.uniform(jax.random.fold_in(jax.random.fold_in(key, 6), dim), (parts,), jnp.float32, smallest / len(cuts), high / len(cuts))
        factor_of = factor_of * jnp.repeat(jnp.exp(steps), dims[dim] // parts).reshape((-1,) + (1,) * (len(dims) - 1 - dim))
    return factor_of


def centred(own_key, extent, spread, limit, cuts=(), held_as=jnp.bfloat16):
    values = jax.random.normal(own_key, extent, jnp.float32) * spread
    if len(cuts) > 0:
        values = shard_levels(own_key, extent, cuts, -0.22, 0.18) * values
    return jnp.clip(values, min=-limit, max=limit).astype(held_as)


def setup_inputs(seed: int = 0) -> dict:
    seeds = jax.random.split(jax.random.key(seed), 7)
    return {
        "spectrum": centred(seeds[0], (4, L, L, NCHEB), 1.0, 6.0, ((1, 8), (2, 4))),
        "radial_table": centred(seeds[1], (NRAD, NCHEB), NCHEB ** -0.5, 0.3125),
        "legendre": centred(seeds[2], (L, L, NTH), (L // 2) ** -0.5, 0.375, ((0, 8), (1, 4))),
        "order_table": jax.random.permutation(seeds[3], L).astype(jnp.int32),
        "cylinder_row": with_ends(jax.random.randint(seeds[4], (NTH, NRAD), 0, NS), jax.random.fold_in(seeds[4], 1), 0, NS - 1).astype(jnp.int32),
        "column_weight": jnp.clip(jnp.exp(math.log(2.0) - 1.3862944 * jax.random.uniform(seeds[5], (NTH, NRAD), jnp.float32) ** shard_levels(seeds[5], (NTH, NRAD), ((0, 32),), -0.2, 0.2)), 0.5, 2.0),
    }


def synthesis_tables(order_table):
    orders = order_table.astype(jnp.int32)
    longitude = jnp.arange(NPHI, dtype=jnp.int32)
    phase_index = orders[:, None] * longitude[None, :] % NPHI
    angles = phase_index.astype(jnp.float32) * (2.0 * math.pi / NPHI)
    weights = jnp.where(orders == 0, 1.0, 2.0).astype(jnp.float32) / math.sqrt(L)
    cosine = jnp.cos(angles) * weights[:, None]
    sine = jnp.sin(angles) * weights[:, None]
    slopes = (orders.astype(jnp.float32) / L)[:, None]
    values = jnp.stack([cosine, -sine])
    turned = jnp.stack([-sine * slopes, -cosine * slopes])
    return jnp.concatenate([values, turned], axis=2).astype(jnp.bfloat16)

def reference(spectrum, radial_table, legendre, order_table, cylinder_row, column_weight):

    def radial(block):
        flat_block = block.reshape(L * L, NCHEB)
        result = jnp.dot(flat_block, radial_table.T, preferred_element_type=jnp.float32)
        return jnp.moveaxis(result.astype(jnp.bfloat16).reshape(L, L, NRAD), 2, 0)
    levels = lax.map(radial, spectrum)
    degrees = jnp.arange(L, dtype=jnp.int32)

    def legendre_slot(operands):
        slot_table, slot_order, slot_coeff = operands
        allowed = (degrees >= slot_order)[:, None]
        masked = jnp.where(allowed, slot_table, jnp.zeros_like(slot_table))
        return jnp.dot(slot_coeff.reshape(4 * NRAD, L), masked, preferred_element_type=jnp.float32)
    sums = lax.map(legendre_slot, (legendre, order_table.astype(jnp.int32), jnp.moveaxis(levels, 2, 0)))
    latitudes = sums.astype(jnp.bfloat16).reshape(L, 2, 2, NRAD, NTH)
    tables = synthesis_tables(order_table)
    synthesis = jnp.einsum('kfirt,ikq->ftrq', latitudes.astype(jnp.float32), tables.astype(jnp.float32))
    synthesis = synthesis.astype(jnp.bfloat16)
    fields = synthesis[..., :NPHI].astype(jnp.float32)
    slope_field = synthesis[..., NPHI:].astype(jnp.float32)
    buoyancy = fields[0] - 0.8 * fields[1]
    weighted = (column_weight[:, :, None] * buoyancy).reshape(NTH * NRAD, NPHI)
    column = jax.ops.segment_sum(weighted, cylinder_row.reshape(-1), num_segments=NS)
    radius = 0.35 + 0.65 * (jnp.arange(NS, dtype=jnp.int32).astype(jnp.float32) + 0.5) / NS
    outward = (jnp.roll(column, -1, axis=1) - jnp.roll(column, 1, axis=1)) / (2.0 * radius[:, None])
    padded = jnp.pad(column, ((1, 1), (0, 0)))
    beside_all = -(padded[2:] - padded[:-2]) * 0.5
    velocity = jnp.stack([outward, beside_all]).astype(jnp.bfloat16).astype(jnp.float32)
    picked = velocity[:, cylinder_row]
    inverse = 1.0 / (0.35 + 0.65 * (cylinder_row.astype(jnp.float32) + 0.5) / NS)
    advected = fields - 0.05 * inverse[None, :, :, None] * (picked[1][None] * slope_field + picked[0][None] * fields)
    return (column, advected)
```

```python
import functools
import math

import jax
import jax.numpy as jnp
from jax import lax
from jax.experimental import pallas as pl
from jax.experimental.pallas import tpu as pltpu
from jax.sharding import PartitionSpec as P

L = 512
NPHI = 1024
QROWS = 16
MESH = pl.DeviceIdType.MESH


time_step = 0.05
composition_weight = 0.8


def synthesis_tables(order_table):
    longitude = jnp.arange(NPHI, dtype=jnp.int32)
    phase_index = order_table[:, None] * longitude[None, :] % NPHI
    angles = phase_index.astype(jnp.float32) * (2.0 * math.pi / NPHI)
    weights = jnp.where(order_table == 0, 1.0, 2.0).astype(jnp.float32) / math.sqrt(L)
    cosine = jnp.cos(angles) * weights[:, None]
    sine = jnp.sin(angles) * weights[:, None]
    slopes = (order_table.astype(jnp.float32) / L)[:, None]
    values = jnp.stack([cosine, -sine])
    turned = jnp.stack([-sine * slopes, -cosine * slopes])
    return jnp.concatenate([values, turned], axis=2).astype(jnp.bfloat16)


def column_kernel(rad_count, ma_count, partial_ref, sum_ref, velocity_ref, arrived, mine, beside, whole,
                  send_a, recv_a, send_b, recv_b, send_c, recv_c):
    r = lax.axis_index("rad")
    m = lax.axis_index("ma")
    total_rows, width = partial_ref.shape
    rows = total_rows // ma_count
    barrier = pltpu.get_barrier_semaphore()
    for d in range(1, ma_count):
        pl.semaphore_signal(
            barrier, inc=1, device_id={"ma": lax.rem(m + d, ma_count)}, device_id_type=MESH
        )
    for d in range(1, rad_count):
        pl.semaphore_signal(
            barrier, inc=1, device_id={"rad": lax.rem(r + d, rad_count)}, device_id_type=MESH
        )
    pl.semaphore_wait(barrier, ma_count + rad_count - 2)

    def block_of(index):
        return pl.ds(pl.multiple_of(index * rows, rows), rows)

    first = []
    for d in range(1, ma_count):
        peer = lax.rem(m + d, ma_count)
        copy = pltpu.make_async_remote_copy(
            src_ref=partial_ref.at[block_of(peer)],
            dst_ref=arrived.at[d - 1],
            send_sem=send_a.at[d - 1],
            recv_sem=recv_a.at[d - 1],
            device_id={"ma": peer},
            device_id_type=MESH,
        )
        copy.start()
        first.append(copy)
    mine[...] = partial_ref[block_of(m), :]
    for d in range(1, ma_count):
        first[d - 1].wait_recv()
        mine[...] += arrived[d - 1]
    second = []
    for d in range(1, rad_count):
        copy = pltpu.make_async_remote_copy(
            src_ref=mine,
            dst_ref=beside.at[d - 1],
            send_sem=send_b.at[d - 1],
            recv_sem=recv_b.at[d - 1],
            device_id={"rad": lax.rem(r + d, rad_count)},
            device_id_type=MESH,
        )
        copy.start()
        second.append(copy)
    total = mine[...]
    for d in range(1, rad_count):
        second[d - 1].wait_recv()
        total = total + beside[d - 1]
    whole[block_of(m), :] = total
    third = []
    for d in range(1, ma_count):
        copy = pltpu.make_async_remote_copy(
            src_ref=whole.at[block_of(m)],
            dst_ref=whole.at[block_of(m)],
            send_sem=send_c.at[d - 1],
            recv_sem=recv_c.at[d - 1],
            device_id={"ma": lax.rem(m + d, ma_count)},
            device_id_type=MESH,
        )
        copy.start()
        third.append(copy)
    sum_ref[...] = total
    for d in range(1, ma_count):
        sender = lax.rem(m + ma_count - d, ma_count)
        pltpu.make_async_remote_copy(
            src_ref=whole.at[block_of(sender)],
            dst_ref=whole.at[block_of(sender)],
            send_sem=send_c.at[d - 1],
            recv_sem=recv_c.at[d - 1],
            device_id={"ma": sender},
            device_id_type=MESH,
        ).wait_recv()
    for copy in first + second + third:
        copy.wait_send()
    value = whole[...]
    row = lax.broadcasted_iota(jnp.int32, (total_rows, 1), 0)
    radius = 0.35 + 0.65 * (row.astype(jnp.float32) + 0.5) / total_rows
    after = pltpu.roll(value, width - 1, 1)
    before = pltpu.roll(value, 1, 1)
    velocity_ref[0] = ((after - before) / (2.0 * radius)).astype(jnp.bfloat16)
    above = jnp.where(row == total_rows - 1, 0.0, pltpu.roll(value, total_rows - 1, 0))
    below = jnp.where(row == 0, 0.0, pltpu.roll(value, 1, 0))
    velocity_ref[1] = (-(above - below) * 0.5).astype(jnp.bfloat16)


def column_exchange(partial_value):
    rad_count = lax.axis_size("rad")
    ma_count = lax.axis_size("ma")
    total_rows, width = partial_value.shape
    rows = total_rows // ma_count
    dma = pltpu.SemaphoreType.DMA
    vmem = pl.BlockSpec(memory_space=pltpu.VMEM)
    summed, velocity = pl.pallas_call(
        functools.partial(column_kernel, rad_count, ma_count),
        out_shape=(
            jax.ShapeDtypeStruct((rows, width), jnp.float32),
            jax.ShapeDtypeStruct((2, total_rows, width), jnp.bfloat16),
        ),
        in_specs=[vmem],
        out_specs=(vmem, vmem),
        scratch_shapes=[
            pltpu.VMEM((ma_count - 1, rows, width), jnp.float32),
            pltpu.VMEM((rows, width), jnp.float32),
            pltpu.VMEM((rad_count - 1, rows, width), jnp.float32),
            pltpu.VMEM((total_rows, width), jnp.float32),
            dma((ma_count - 1,)),
            dma((ma_count - 1,)),
            dma((rad_count - 1,)),
            dma((rad_count - 1,)),
            dma((ma_count - 1,)),
            dma((ma_count - 1,)),
        ],
        compiler_params=pltpu.CompilerParams(collective_id=0, has_side_effects=True),
        name="column_exchange",
    )(partial_value)
    block = width // rad_count
    owned = lax.dynamic_slice_in_dim(summed, lax.axis_index("rad") * block, block, axis=1)
    return owned, velocity


def on_device(spectrum, radial_table, legendre, order_table, cylinder_row, column_weight):
    slot_count = spectrum.shape[1]
    degree_count = spectrum.shape[2]
    level_count = radial_table.shape[0]
    latitude_count = legendre.shape[2]
    rad_count = lax.axis_size("rad")
    ma_count = lax.axis_size("ma")
    total_rows = QROWS * ma_count
    my_orders = lax.dynamic_slice_in_dim(order_table, lax.axis_index("ma") * slot_count, slot_count)
    my_degrees = lax.axis_index("rad") * degree_count + jnp.arange(degree_count, dtype=jnp.int32)
    allowed = my_degrees[None, :] >= my_orders[:, None]
    masked_table = jnp.where(allowed[:, :, None], legendre, jnp.zeros_like(legendre))
    levels = jnp.einsum(
        "rn,ckln->rckl", radial_table, spectrum, preferred_element_type=jnp.float32
    ).astype(jnp.bfloat16)
    contribution = jnp.einsum(
        "klt,rckl->trck", masked_table, levels, preferred_element_type=jnp.float32
    )
    pieces = contribution.astype(jnp.bfloat16).reshape(
        rad_count, latitude_count // rad_count, level_count * 4 * slot_count
    )
    pieces = lax.all_to_all(pieces, "rad", split_axis=0, concat_axis=0, tiled=True)
    latitudes = jnp.sum(pieces.astype(jnp.float32), axis=0).astype(jnp.bfloat16)
    received = lax.all_to_all(latitudes, "ma", split_axis=0, concat_axis=1, tiled=True)
    lat_rows = received.shape[0]
    coefficients = received.reshape(lat_rows, ma_count, level_count, 2, 2, slot_count)
    tables = synthesis_tables(order_table).reshape(2, ma_count, slot_count, 2 * NPHI)
    synthesis = jnp.einsum(
        "tsrfik,iskq->ftrq", coefficients, tables, preferred_element_type=jnp.float32
    ).astype(jnp.bfloat16)
    fields = synthesis[..., :NPHI].astype(jnp.float32)
    slope_field = synthesis[..., NPHI:].astype(jnp.float32)
    buoyancy = fields[0] - composition_weight * fields[1]
    weighted = (column_weight[:, :, None] * buoyancy).reshape(-1, NPHI)
    point_rows = cylinder_row.reshape(-1)
    row_ids = jnp.arange(total_rows, dtype=jnp.int32)
    selector = (row_ids[:, None] == point_rows[None, :]).astype(jnp.float32)
    partial_value = jnp.dot(
        selector, weighted, precision=lax.Precision.HIGHEST, preferred_element_type=jnp.float32
    )
    owned, velocity = column_exchange(partial_value)
    chooser = (point_rows[:, None] == row_ids[None, :]).astype(jnp.bfloat16)
    moved = jnp.einsum("pj,cjq->cpq", chooser, velocity, preferred_element_type=jnp.float32)
    moved = moved.reshape(2, lat_rows, level_count, NPHI)
    inverse = 1.0 / (0.35 + 0.65 * (cylinder_row.astype(jnp.float32) + 0.5) / total_rows)
    advected = fields - time_step * inverse[None, :, :, None] * (
        moved[1][None] * slope_field + moved[0][None] * fields
    )
    return (owned, advected)


def solution(mesh):
    return jax.shard_map(
        on_device,
        mesh=mesh,
        in_specs=(
            P(None, "ma", "rad", None),
            P(),
            P("ma", "rad", None),
            P(),
            P(("rad", "ma"), None),
            P(("rad", "ma"), None),
        ),
        out_specs=(P("ma", "rad"), P(None, ("rad", "ma"), None, None)),
        check_vma=False,
    )
```

```python
import functools
import math

import jax
import jax.numpy as jnp
from jax import lax
from jax.experimental import pallas as pl
from jax.experimental.pallas import tpu as pltpu
from jax.sharding import PartitionSpec as P

L = 512
NPHI = 1024
QROWS = 16
LANES = 128
GROUP = 8
MESH = pl.DeviceIdType.MESH


time_step = 0.05
composition_weight = 0.8


def synthesis_tables(order_table):
    def turn(steps):
        phase_index = order_table[:, None] * steps[None, :] % NPHI
        angles = phase_index.astype(jnp.float32) * (2.0 * math.pi / NPHI)
        return jnp.cos(angles), jnp.sin(angles)

    near_cos, near_sin = turn(jnp.arange(LANES, dtype=jnp.int32))
    far_cos, far_sin = turn(jnp.arange(NPHI // LANES, dtype=jnp.int32) * LANES)
    weights = jnp.where(order_table == 0, 1.0, 2.0).astype(jnp.float32) / math.sqrt(L)
    far_cos = (far_cos * weights[:, None])[:, :, None]
    far_sin = (far_sin * weights[:, None])[:, :, None]
    near_cos = near_cos[:, None, :]
    near_sin = near_sin[:, None, :]
    cosine = far_cos * near_cos - far_sin * near_sin
    sine = far_sin * near_cos + far_cos * near_sin
    slopes = (order_table.astype(jnp.float32) / L)[:, None, None]
    values = jnp.stack([cosine, -sine])
    turned = jnp.stack([-sine * slopes, -cosine * slopes])
    tables = jnp.concatenate([values, turned], axis=2).astype(jnp.bfloat16)
    return tables.reshape(2, order_table.shape[0], 2 * NPHI)


def latitude_kernel(rad_count, ma_count, chunks, mask_ref, radial_ref, spectrum_ref, legendre_ref, out_ref,
                    spectrum_buf, legendre_buf, own, out_up, out_down, in_up, in_down, ready, arrived,
                    fetch_sem, up_send, up_recv, down_send, down_recv, ma_send, ma_recv):
    r = lax.axis_index("rad")
    m = lax.axis_index("ma")
    last = rad_count - 1
    _, _, slots, degrees, modes = spectrum_buf.shape
    rows = radial_ref.shape[1]
    lanes = own.shape[3]
    share = out_ref.shape[2]

    def fetch(c, slot):
        piece = pl.ds(c * slots, slots)
        return (
            pltpu.make_async_copy(
                spectrum_ref.at[:, piece], spectrum_buf.at[slot], fetch_sem.at[0, slot]
            ),
            pltpu.make_async_copy(
                legendre_ref.at[piece], legendre_buf.at[slot], fetch_sem.at[1, slot]
            ),
        )

    for copy in fetch(0, 0):
        copy.start()

    barrier = pltpu.get_barrier_semaphore()
    for d in range(1, ma_count):
        pl.semaphore_signal(
            barrier, inc=1, device_id={"ma": lax.rem(m + d, ma_count)}, device_id_type=MESH
        )
    for d in range(1, rad_count):
        pl.semaphore_signal(
            barrier, inc=1, device_id={"rad": lax.rem(r + d, rad_count)}, device_id_type=MESH
        )
    pl.semaphore_wait(barrier, ma_count + rad_count - 2)

    def up(c, target):
        return pltpu.make_async_remote_copy(
            src_ref=out_up.at[c, target],
            dst_ref=in_up.at[c, target],
            send_sem=up_send.at[c, target],
            recv_sem=up_recv.at[c, target],
            device_id={"rad": lax.rem(r + 1, rad_count)},
            device_id_type=MESH,
        )

    def down(c, target):
        return pltpu.make_async_remote_copy(
            src_ref=out_down.at[c, target],
            dst_ref=in_down.at[c, target],
            send_sem=down_send.at[c, target],
            recv_sem=down_recv.at[c, target],
            device_id={"rad": lax.rem(r + last, rad_count)},
            device_id_type=MESH,
        )

    def hand_over(c, d):
        peer = lax.rem(m + d, ma_count)
        return pltpu.make_async_remote_copy(
            src_ref=ready.at[c, pl.ds(pl.multiple_of(peer * share, share), share)],
            dst_ref=arrived.at[m, c],
            send_sem=ma_send.at[c, d - 1],
            recv_sem=ma_recv.at[c, d - 1],
            device_id={"ma": peer},
            device_id_type=MESH,
        )

    def compute(c, carry):
        slot = lax.rem(c, 2)

        @pl.when(c + 1 < chunks)
        def _():
            for copy in fetch(c + 1, 1 - slot):
                copy.start()

        for copy in fetch(c, slot):
            copy.wait()
        levels = jnp.zeros((rows, slots * degrees), jnp.float32)
        for part in range(spectrum_buf.shape[1]):
            levels += lax.dot_general(
                radial_ref[part],
                spectrum_buf[slot, part].reshape(slots * degrees, modes),
                (((1,), (1,)), ((), ())),
                preferred_element_type=jnp.float32,
            )
        for s in range(slots):
            kept = levels[:, s * degrees : (s + 1) * degrees] * mask_ref[c * slots + s]
            sums = jnp.dot(
                kept.astype(jnp.bfloat16), legendre_buf[slot, s], preferred_element_type=jnp.float32
            )
            for target in range(rad_count):
                own[c, target, s * rows : (s + 1) * rows, :] = sums[
                    :, target * lanes : (target + 1) * lanes
                ]

        @pl.when(r == 0)
        def _():
            for target in range(last, 0, -1):
                out_up[c, target] = own[c, target].astype(jnp.bfloat16)
                up(c, target).start()

        @pl.when(r == last)
        def _():
            for target in range(last):
                out_down[c, target] = own[c, target].astype(jnp.bfloat16)
                down(c, target).start()

        return carry

    lax.fori_loop(0, chunks, compute, 0)

    def relay(c):
        for target in range(last, 0, -1):

            @pl.when((r > 0) & (r < target))
            def _():
                up(c, target).wait_recv()
                out_up[c, target] = (
                    own[c, target] + in_up[c, target].astype(jnp.float32)
                ).astype(jnp.bfloat16)
                up(c, target).start()

        for target in range(last):

            @pl.when((r < last) & (r > target))
            def _():
                down(c, target).wait_recv()
                out_down[c, target] = (
                    own[c, target] + in_down[c, target].astype(jnp.float32)
                ).astype(jnp.bfloat16)
                down(c, target).start()

    def finish(c):
        @pl.when(r > 0)
        def _():
            up(c, r).wait_recv()
            own[c, r] += in_up[c, r].astype(jnp.float32)

        @pl.when(r < last)
        def _():
            down(c, r).wait_recv()
            own[c, r] += in_down[c, r].astype(jnp.float32)

        ready[c] = own[c, r].T.astype(jnp.bfloat16)
        for d in range(1, ma_count):
            hand_over(c, d).start()
        arrived[m, c] = ready[c, pl.ds(pl.multiple_of(m * share, share), share), :]

    def pass_on(c, carry):
        relay(c)

        @pl.when(c > 0)
        def _():
            finish(c - 1)

        return carry

    lax.fori_loop(0, chunks, pass_on, 0)
    finish(chunks - 1)

    def drain(c, carry):
        for d in range(1, ma_count):
            sender = lax.rem(m + ma_count - d, ma_count)
            pltpu.make_async_remote_copy(
                src_ref=ready.at[c, pl.ds(0, share)],
                dst_ref=arrived.at[sender, c],
                send_sem=ma_send.at[c, d - 1],
                recv_sem=ma_recv.at[c, d - 1],
                device_id={"ma": sender},
                device_id_type=MESH,
            ).wait_recv()
            hand_over(c, d).wait_send()
        for target in range(rad_count):

            @pl.when(r < target)
            def _():
                up(c, target).wait_send()

            @pl.when(r > target)
            def _():
                down(c, target).wait_send()

        return carry

    lax.fori_loop(0, chunks, drain, 0)
    out_ref[...] = arrived[...]


def latitude_exchange(spectrum, radial_table, legendre, allowed, slots):
    rad_count = lax.axis_size("rad")
    ma_count = lax.axis_size("ma")
    parts, slot_count, degrees, modes = spectrum.shape
    level_count = radial_table.shape[0]
    latitude_count = legendre.shape[2]
    rows = level_count * parts
    chunks = slot_count // slots
    lanes = latitude_count // rad_count
    share = lanes // ma_count
    spread = jnp.einsum("rn,cd->crdn", radial_table, jnp.eye(parts, dtype=radial_table.dtype))
    spread = spread.reshape(parts, rows, modes)
    dma = pltpu.SemaphoreType.DMA
    vmem = pl.BlockSpec(memory_space=pltpu.VMEM)
    hbm = pl.BlockSpec(memory_space=pl.ANY)
    travelling = pltpu.VMEM((chunks, rad_count, slots * rows, lanes), jnp.bfloat16)
    return pl.pallas_call(
        functools.partial(latitude_kernel, rad_count, ma_count, chunks),
        out_shape=jax.ShapeDtypeStruct((ma_count, chunks, share, slots * rows), jnp.bfloat16),
        in_specs=[vmem, vmem, hbm, hbm],
        out_specs=vmem,
        scratch_shapes=[
            pltpu.VMEM((2, parts, slots, degrees, modes), jnp.bfloat16),
            pltpu.VMEM((2, slots, degrees, latitude_count), jnp.bfloat16),
            pltpu.VMEM((chunks, rad_count, slots * rows, lanes), jnp.float32),
            travelling,
            travelling,
            travelling,
            travelling,
            pltpu.VMEM((chunks, lanes, slots * rows), jnp.bfloat16),
            pltpu.VMEM((ma_count, chunks, share, slots * rows), jnp.bfloat16),
            dma((2, 2)),
            dma((chunks, rad_count)),
            dma((chunks, rad_count)),
            dma((chunks, rad_count)),
            dma((chunks, rad_count)),
            dma((chunks, ma_count - 1)),
            dma((chunks, ma_count - 1)),
        ],
        compiler_params=pltpu.CompilerParams(
            collective_id=1, has_side_effects=True, vmem_limit_bytes=56 * 1024 * 1024
        ),
        name="latitude_exchange",
    )(allowed.astype(jnp.float32)[:, None, :], spread, spectrum, legendre)


def column_kernel(rad_count, ma_count, partial_ref, sum_ref, velocity_ref, arrived, mine, beside, whole,
                  send_a, recv_a, send_b, recv_b, send_c, recv_c):
    r = lax.axis_index("rad")
    m = lax.axis_index("ma")
    total_rows, width = partial_ref.shape
    rows = total_rows // ma_count
    barrier = pltpu.get_barrier_semaphore()
    for d in range(1, ma_count):
        pl.semaphore_signal(
            barrier, inc=1, device_id={"ma": lax.rem(m + d, ma_count)}, device_id_type=MESH
        )
    for d in range(1, rad_count):
        pl.semaphore_signal(
            barrier, inc=1, device_id={"rad": lax.rem(r + d, rad_count)}, device_id_type=MESH
        )
    pl.semaphore_wait(barrier, ma_count + rad_count - 2)

    def block_of(index):
        return pl.ds(pl.multiple_of(index * rows, rows), rows)

    first = []
    for d in range(1, ma_count):
        peer = lax.rem(m + d, ma_count)
        copy = pltpu.make_async_remote_copy(
            src_ref=partial_ref.at[block_of(peer)],
            dst_ref=arrived.at[d - 1],
            send_sem=send_a.at[d - 1],
            recv_sem=recv_a.at[d - 1],
            device_id={"ma": peer},
            device_id_type=MESH,
        )
        copy.start()
        first.append(copy)
    mine[...] = partial_ref[block_of(m), :]
    for d in range(1, ma_count):
        first[d - 1].wait_recv()
        mine[...] += arrived[d - 1]
    second = []
    for d in range(1, rad_count):
        copy = pltpu.make_async_remote_copy(
            src_ref=mine,
            dst_ref=beside.at[d - 1],
            send_sem=send_b.at[d - 1],
            recv_sem=recv_b.at[d - 1],
            device_id={"rad": lax.rem(r + d, rad_count)},
            device_id_type=MESH,
        )
        copy.start()
        second.append(copy)
    total = mine[...]
    for d in range(1, rad_count):
        second[d - 1].wait_recv()
        total = total + beside[d - 1]
    whole[block_of(m), :] = total
    third = []
    for d in range(1, ma_count):
        copy = pltpu.make_async_remote_copy(
            src_ref=whole.at[block_of(m)],
            dst_ref=whole.at[block_of(m)],
            send_sem=send_c.at[d - 1],
            recv_sem=recv_c.at[d - 1],
            device_id={"ma": lax.rem(m + d, ma_count)},
            device_id_type=MESH,
        )
        copy.start()
        third.append(copy)
    sum_ref[...] = total
    for d in range(1, ma_count):
        sender = lax.rem(m + ma_count - d, ma_count)
        pltpu.make_async_remote_copy(
            src_ref=whole.at[block_of(sender)],
            dst_ref=whole.at[block_of(sender)],
            send_sem=send_c.at[d - 1],
            recv_sem=recv_c.at[d - 1],
            device_id={"ma": sender},
            device_id_type=MESH,
        ).wait_recv()
    for copy in first + second + third:
        copy.wait_send()
    value = whole[...]
    row = lax.broadcasted_iota(jnp.int32, (total_rows, 1), 0)
    radius = 0.35 + 0.65 * (row.astype(jnp.float32) + 0.5) / total_rows
    after = pltpu.roll(value, width - 1, 1)
    before = pltpu.roll(value, 1, 1)
    velocity_ref[0] = ((after - before) / (2.0 * radius)).astype(jnp.bfloat16)
    above = jnp.where(row == total_rows - 1, 0.0, pltpu.roll(value, total_rows - 1, 0))
    below = jnp.where(row == 0, 0.0, pltpu.roll(value, 1, 0))
    velocity_ref[1] = (-(above - below) * 0.5).astype(jnp.bfloat16)


def column_exchange(partial_value):
    rad_count = lax.axis_size("rad")
    ma_count = lax.axis_size("ma")
    total_rows, width = partial_value.shape
    rows = total_rows // ma_count
    dma = pltpu.SemaphoreType.DMA
    vmem = pl.BlockSpec(memory_space=pltpu.VMEM)
    summed, velocity = pl.pallas_call(
        functools.partial(column_kernel, rad_count, ma_count),
        out_shape=(
            jax.ShapeDtypeStruct((rows, width), jnp.float32),
            jax.ShapeDtypeStruct((2, total_rows, width), jnp.bfloat16),
        ),
        in_specs=[vmem],
        out_specs=(vmem, vmem),
        scratch_shapes=[
            pltpu.VMEM((ma_count - 1, rows, width), jnp.float32),
            pltpu.VMEM((rows, width), jnp.float32),
            pltpu.VMEM((rad_count - 1, rows, width), jnp.float32),
            pltpu.VMEM((total_rows, width), jnp.float32),
            dma((ma_count - 1,)),
            dma((ma_count - 1,)),
            dma((rad_count - 1,)),
            dma((rad_count - 1,)),
            dma((ma_count - 1,)),
            dma((ma_count - 1,)),
        ],
        compiler_params=pltpu.CompilerParams(collective_id=0, has_side_effects=True),
        name="column_exchange",
    )(partial_value)
    block = width // rad_count
    owned = lax.dynamic_slice_in_dim(summed, lax.axis_index("rad") * block, block, axis=1)
    return owned, velocity


def on_device(spectrum, radial_table, legendre, order_table, cylinder_row, column_weight):
    slot_count = spectrum.shape[1]
    degree_count = spectrum.shape[2]
    level_count = radial_table.shape[0]
    latitude_count = legendre.shape[2]
    rad_count = lax.axis_size("rad")
    ma_count = lax.axis_size("ma")
    total_rows = QROWS * ma_count
    my_orders = lax.dynamic_slice_in_dim(order_table, lax.axis_index("ma") * slot_count, slot_count)
    my_degrees = lax.axis_index("rad") * degree_count + jnp.arange(degree_count, dtype=jnp.int32)
    allowed = my_degrees[None, :] >= my_orders[:, None]
    tables = synthesis_tables(order_table)
    lat_rows = latitude_count // (rad_count * ma_count)
    if (
        latitude_count % (rad_count * LANES) == 0
        and degree_count % LANES == 0
        and slot_count % GROUP == 0
        and GROUP * level_count * 4 % LANES == 0
        and lat_rows % 16 == 0
    ):
        received = latitude_exchange(spectrum, radial_table, legendre, allowed, GROUP)
        coefficients = received.reshape(
            ma_count, slot_count // GROUP, lat_rows, GROUP, level_count, 2, 2
        )
        coefficients = coefficients.transpose(2, 4, 5, 6, 0, 1, 3)
        coefficients = coefficients.reshape(lat_rows, level_count, 2, 2, ma_count * slot_count)
    else:
        masked_table = jnp.where(allowed[:, :, None], legendre, jnp.zeros_like(legendre))
        levels = jnp.einsum(
            "rn,ckln->rckl", radial_table, spectrum, preferred_element_type=jnp.float32
        ).astype(jnp.bfloat16)
        contribution = jnp.einsum(
            "klt,rckl->trck", masked_table, levels, preferred_element_type=jnp.float32
        )
        pieces = contribution.astype(jnp.bfloat16).reshape(
            rad_count, latitude_count // rad_count, level_count * 4 * slot_count
        )
        pieces = lax.all_to_all(pieces, "rad", split_axis=0, concat_axis=0, tiled=True)
        latitudes = jnp.sum(pieces.astype(jnp.float32), axis=0).astype(jnp.bfloat16)
        received = lax.all_to_all(latitudes, "ma", split_axis=0, concat_axis=1, tiled=True)
        coefficients = received.reshape(lat_rows, ma_count, level_count, 2, 2, slot_count)
        coefficients = coefficients.transpose(0, 2, 3, 4, 1, 5)
        coefficients = coefficients.reshape(lat_rows, level_count, 2, 2, ma_count * slot_count)
    synthesis = jnp.einsum(
        "trfik,ikq->ftrq", coefficients, tables, preferred_element_type=jnp.float32
    ).astype(jnp.bfloat16)
    fields = synthesis[..., :NPHI].astype(jnp.float32)
    slope_field = synthesis[..., NPHI:].astype(jnp.float32)
    buoyancy = fields[0] - composition_weight * fields[1]
    weighted = (column_weight[:, :, None] * buoyancy).reshape(-1, NPHI)
    point_rows = cylinder_row.reshape(-1)
    row_ids = jnp.arange(total_rows, dtype=jnp.int32)
    selector = (row_ids[:, None] == point_rows[None, :]).astype(jnp.float32)
    partial_value = jnp.dot(
        selector, weighted, precision=lax.Precision.HIGHEST, preferred_element_type=jnp.float32
    )
    owned, velocity = column_exchange(partial_value)
    chooser = (point_rows[:, None] == row_ids[None, :]).astype(jnp.bfloat16)
    moved = jnp.einsum("pj,cjq->cpq", chooser, velocity, preferred_element_type=jnp.float32)
    moved = moved.reshape(2, lat_rows, level_count, NPHI)
    inverse = 1.0 / (0.35 + 0.65 * (cylinder_row.astype(jnp.float32) + 0.5) / total_rows)
    advected = fields - time_step * inverse[None, :, :, None] * (
        moved[1][None] * slope_field + moved[0][None] * fields
    )
    return (owned, advected)


def solution(mesh):
    return jax.shard_map(
        on_device,
        mesh=mesh,
        in_specs=(
            P(None, "ma", "rad", None),
            P(),
            P("ma", "rad", None),
            P(),
            P(("rad", "ma"), None),
            P(("rad", "ma"), None),
        ),
        out_specs=(P("ma", "rad"), P(None, ("rad", "ma"), None, None)),
        check_vma=False,
    )
```

```python
import functools
import math

import jax
import jax.numpy as jnp
from jax import lax
from jax.experimental import pallas as pl
from jax.experimental.pallas import tpu as pltpu
from jax.sharding import PartitionSpec as P

L = 512
NPHI = 1024
QROWS = 16
LANES = 128
GROUP = 8
HALVES = 2
MESH = pl.DeviceIdType.MESH


time_step = 0.05
composition_weight = 0.8


def synthesis_tables(order_table):
    def turn(steps):
        phase_index = order_table[:, None] * steps[None, :] % NPHI
        angles = phase_index.astype(jnp.float32) * (2.0 * math.pi / NPHI)
        return jnp.cos(angles), jnp.sin(angles)

    near_cos, near_sin = turn(jnp.arange(LANES, dtype=jnp.int32))
    far_cos, far_sin = turn(jnp.arange(NPHI // LANES, dtype=jnp.int32) * LANES)
    weights = jnp.where(order_table == 0, 1.0, 2.0).astype(jnp.float32) / math.sqrt(L)
    far_cos = far_cos * weights[:, None]
    far_sin = far_sin * weights[:, None]
    slopes = (order_table.astype(jnp.float32) / L)[:, None]
    count = order_table.shape[0]
    block = 64
    columns = far_cos.shape[1]
    near = pl.BlockSpec((block, LANES), lambda i: (i, 0))
    far = pl.BlockSpec((block, columns), lambda i: (i, 0))
    return pl.pallas_call(
        table_kernel,
        grid=(count // block,),
        out_shape=jax.ShapeDtypeStruct((2, count, 2 * NPHI), jnp.bfloat16),
        in_specs=[near, near, far, far, pl.BlockSpec((block, 1), lambda i: (i, 0))],
        out_specs=pl.BlockSpec((2, block, 2 * NPHI), lambda i: (0, i, 0)),
        name="tables",
    )(near_cos, near_sin, far_cos, far_sin, slopes)


def table_kernel(near_cos_ref, near_sin_ref, far_cos_ref, far_sin_ref, slope_ref, out_ref):
    near_cos = near_cos_ref[...]
    near_sin = near_sin_ref[...]
    slope = slope_ref[...]
    for a in range(far_cos_ref.shape[1]):
        far_cos = far_cos_ref[:, a : a + 1]
        far_sin = far_sin_ref[:, a : a + 1]
        cosine = far_cos * near_cos - far_sin * near_sin
        sine = far_sin * near_cos + far_cos * near_sin
        value = slice(a * LANES, (a + 1) * LANES)
        turned = slice(NPHI + a * LANES, NPHI + (a + 1) * LANES)
        out_ref[0, :, value] = cosine.astype(jnp.bfloat16)
        out_ref[1, :, value] = (-sine).astype(jnp.bfloat16)
        out_ref[0, :, turned] = (-sine * slope).astype(jnp.bfloat16)
        out_ref[1, :, turned] = (-cosine * slope).astype(jnp.bfloat16)


def latitude_kernel(rad_count, ma_count, chunks, mask_ref, radial_ref, spectrum_ref, legendre_ref, out_ref,
                    spectrum_buf, legendre_buf, own, out_up, out_down, in_up, in_down, finished, ready, arrived,
                    fetch_sem, up_send, up_recv, down_send, down_recv, ma_send, ma_recv):
    r = lax.axis_index("rad")
    m = lax.axis_index("ma")
    last = rad_count - 1
    _, _, slots, degrees, modes = spectrum_buf.shape
    rows = radial_ref.shape[1]
    lanes = own.shape[3]
    share = out_ref.shape[0]

    def fetch(c, slot):
        piece = pl.ds(c * slots, slots)
        return (
            pltpu.make_async_copy(
                spectrum_ref.at[:, piece], spectrum_buf.at[slot], fetch_sem.at[0, slot]
            ),
            pltpu.make_async_copy(
                legendre_ref.at[piece], legendre_buf.at[slot], fetch_sem.at[1, slot]
            ),
        )

    for copy in fetch(0, 0):
        copy.start()

    barrier = pltpu.get_barrier_semaphore()
    for d in range(1, ma_count):
        pl.semaphore_signal(
            barrier, inc=1, device_id={"ma": lax.rem(m + d, ma_count)}, device_id_type=MESH
        )
    for d in range(1, rad_count):
        pl.semaphore_signal(
            barrier, inc=1, device_id={"rad": lax.rem(r + d, rad_count)}, device_id_type=MESH
        )
    pl.semaphore_wait(barrier, ma_count + rad_count - 2)

    def up(c, target):
        return pltpu.make_async_remote_copy(
            src_ref=out_up.at[c, target],
            dst_ref=in_up.at[c, target],
            send_sem=up_send.at[c, target],
            recv_sem=up_recv.at[c, target],
            device_id={"rad": lax.rem(r + 1, rad_count)},
            device_id_type=MESH,
        )

    def down(c, target):
        return pltpu.make_async_remote_copy(
            src_ref=out_down.at[c, target],
            dst_ref=in_down.at[c, target],
            send_sem=down_send.at[c, target],
            recv_sem=down_recv.at[c, target],
            device_id={"rad": lax.rem(r + last, rad_count)},
            device_id_type=MESH,
        )

    half_chunks = chunks // HALVES
    kept_slots = half_chunks * slots
    width = rows * kept_slots

    def landing(source, h):
        start = (source * HALVES + h) * width
        return arrived.at[:, pl.ds(pl.multiple_of(start, width), width)]

    def hand_over(h, d):
        peer = lax.rem(m + d, ma_count)
        return pltpu.make_async_remote_copy(
            src_ref=ready.at[h, pl.ds(pl.multiple_of(peer * share, share), share)],
            dst_ref=landing(m, h),
            send_sem=ma_send.at[h, d - 1],
            recv_sem=ma_recv.at[h, d - 1],
            device_id={"ma": peer},
            device_id_type=MESH,
        )

    def compute(c, carry):
        slot = lax.rem(c, 2)

        @pl.when(c + 1 < chunks)
        def _():
            for copy in fetch(c + 1, 1 - slot):
                copy.start()

        for copy in fetch(c, slot):
            copy.wait()
        levels = jnp.zeros((rows, slots * degrees), jnp.float32)
        for part in range(spectrum_buf.shape[1]):
            levels += lax.dot_general(
                radial_ref[part],
                spectrum_buf[slot, part].reshape(slots * degrees, modes),
                (((1,), (1,)), ((), ())),
                preferred_element_type=jnp.float32,
            )
        for s in range(slots):
            kept = levels[:, s * degrees : (s + 1) * degrees] * mask_ref[c * slots + s]
            sums = jnp.dot(
                kept.astype(jnp.bfloat16), legendre_buf[slot, s], preferred_element_type=jnp.float32
            )
            for target in range(rad_count):
                own[c, target, s * rows : (s + 1) * rows, :] = sums[
                    :, target * lanes : (target + 1) * lanes
                ]

        @pl.when(r == 0)
        def _():
            for target in range(last, 0, -1):
                out_up[c, target] = own[c, target].astype(jnp.bfloat16)
                up(c, target).start()

        @pl.when(r == last)
        def _():
            for target in range(last):
                out_down[c, target] = own[c, target].astype(jnp.bfloat16)
                down(c, target).start()

        return carry

    lax.fori_loop(0, chunks, compute, 0)

    def relay_up(step, here):
        c = step - (r - 1)
        for target in range(last, 0, -1):

            @pl.when(here & (r > 0) & (r < target) & (c >= 0) & (c < chunks))
            def _():
                up(c, target).wait_recv()
                out_up[c, target] = (
                    own[c, target] + in_up[c, target].astype(jnp.float32)
                ).astype(jnp.bfloat16)
                up(c, target).start()

    def relay_down(step, here):
        c = step - (last - r - 1)
        for target in range(last):

            @pl.when(here & (r < last) & (r > target) & (c >= 0) & (c < chunks))
            def _():
                down(c, target).wait_recv()
                out_down[c, target] = (
                    own[c, target] + in_down[c, target].astype(jnp.float32)
                ).astype(jnp.bfloat16)
                down(c, target).start()

    def finish(c):
        @pl.when(r > 0)
        def _():
            up(c, r).wait_recv()
            own[c, r] += in_up[c, r].astype(jnp.float32)

        @pl.when(r < last)
        def _():
            down(c, r).wait_recv()
            own[c, r] += in_down[c, r].astype(jnp.float32)

        first = lax.rem(c, half_chunks) * slots
        for s in range(slots):
            finished[pl.ds(first + s, rows, stride=kept_slots), :] = own[
                c, r, s * rows : (s + 1) * rows, :
            ]

        @pl.when(lax.rem(c, half_chunks) == half_chunks - 1)
        def _():
            h = c // half_chunks
            ready[h] = finished[...].T.astype(jnp.bfloat16)
            for d in range(1, ma_count):
                hand_over(h, d).start()
            place = pl.ds(pl.multiple_of((m * HALVES + h) * width, width), width)
            arrived[:, place] = ready[h, pl.ds(pl.multiple_of(m * share, share), share), :]

    nearer_top = 2 * r > last
    nearer_bottom = 2 * r <= last

    def pass_on(step, carry):
        relay_up(step, nearer_top)
        relay_down(step, nearer_bottom)
        relay_up(step, nearer_bottom)
        relay_down(step, nearer_top)

        @pl.when(step >= last - 1)
        def _():
            finish(step - (last - 1))

        return carry

    lax.fori_loop(0, chunks + last - 1, pass_on, 0)

    for h in range(HALVES):
        for d in range(1, ma_count):
            sender = lax.rem(m + ma_count - d, ma_count)
            pltpu.make_async_remote_copy(
                src_ref=ready.at[h, pl.ds(0, share)],
                dst_ref=landing(sender, h),
                send_sem=ma_send.at[h, d - 1],
                recv_sem=ma_recv.at[h, d - 1],
                device_id={"ma": sender},
                device_id_type=MESH,
            ).wait_recv()
            hand_over(h, d).wait_send()

    def drain(c, carry):
        for target in range(rad_count):

            @pl.when(r < target)
            def _():
                up(c, target).wait_send()

            @pl.when(r > target)
            def _():
                down(c, target).wait_send()

        return carry

    lax.fori_loop(0, chunks, drain, 0)
    out_ref[...] = arrived[...]


def latitude_exchange(spectrum, radial_table, legendre, allowed, slots):
    rad_count = lax.axis_size("rad")
    ma_count = lax.axis_size("ma")
    parts, slot_count, degrees, modes = spectrum.shape
    level_count = radial_table.shape[0]
    latitude_count = legendre.shape[2]
    rows = level_count * parts
    chunks = slot_count // slots
    lanes = latitude_count // rad_count
    share = lanes // ma_count
    spread = jnp.einsum("rn,cd->crdn", radial_table, jnp.eye(parts, dtype=radial_table.dtype))
    spread = spread.reshape(parts, rows, modes)
    dma = pltpu.SemaphoreType.DMA
    vmem = pl.BlockSpec(memory_space=pltpu.VMEM)
    hbm = pl.BlockSpec(memory_space=pl.ANY)
    travelling = pltpu.VMEM((chunks, rad_count, slots * rows, lanes), jnp.bfloat16)
    return pl.pallas_call(
        functools.partial(latitude_kernel, rad_count, ma_count, chunks),
        out_shape=jax.ShapeDtypeStruct((share, ma_count * rows * slot_count), jnp.bfloat16),
        in_specs=[vmem, vmem, hbm, hbm],
        out_specs=vmem,
        scratch_shapes=[
            pltpu.VMEM((2, parts, slots, degrees, modes), jnp.bfloat16),
            pltpu.VMEM((2, slots, degrees, latitude_count), jnp.bfloat16),
            pltpu.VMEM((chunks, rad_count, slots * rows, lanes), jnp.float32),
            travelling,
            travelling,
            travelling,
            travelling,
            pltpu.VMEM((rows * slot_count // HALVES, lanes), jnp.float32),
            pltpu.VMEM((HALVES, lanes, rows * slot_count // HALVES), jnp.bfloat16),
            pltpu.VMEM((share, ma_count * rows * slot_count), jnp.bfloat16),
            dma((2, 2)),
            dma((chunks, rad_count)),
            dma((chunks, rad_count)),
            dma((chunks, rad_count)),
            dma((chunks, rad_count)),
            dma((HALVES, ma_count - 1)),
            dma((HALVES, ma_count - 1)),
        ],
        compiler_params=pltpu.CompilerParams(
            collective_id=1, has_side_effects=True, vmem_limit_bytes=56 * 1024 * 1024
        ),
        name="latitude_exchange",
    )(allowed.astype(jnp.float32)[:, None, :], spread, spectrum, legendre)


def column_kernel(rad_count, ma_count, partial_ref, sum_ref, velocity_ref, arrived, mine, beside, whole,
                  send_a, recv_a, send_b, recv_b, send_c, recv_c):
    r = lax.axis_index("rad")
    m = lax.axis_index("ma")
    total_rows, width = partial_ref.shape
    rows = total_rows // ma_count
    barrier = pltpu.get_barrier_semaphore()
    for d in range(1, ma_count):
        pl.semaphore_signal(
            barrier, inc=1, device_id={"ma": lax.rem(m + d, ma_count)}, device_id_type=MESH
        )
    for d in range(1, rad_count):
        pl.semaphore_signal(
            barrier, inc=1, device_id={"rad": lax.rem(r + d, rad_count)}, device_id_type=MESH
        )
    pl.semaphore_wait(barrier, ma_count + rad_count - 2)

    def block_of(index):
        return pl.ds(pl.multiple_of(index * rows, rows), rows)

    first = []
    for d in range(1, ma_count):
        peer = lax.rem(m + d, ma_count)
        copy = pltpu.make_async_remote_copy(
            src_ref=partial_ref.at[block_of(peer)],
            dst_ref=arrived.at[d - 1],
            send_sem=send_a.at[d - 1],
            recv_sem=recv_a.at[d - 1],
            device_id={"ma": peer},
            device_id_type=MESH,
        )
        copy.start()
        first.append(copy)
    mine[...] = partial_ref[block_of(m), :]
    for d in range(1, ma_count):
        first[d - 1].wait_recv()
        mine[...] += arrived[d - 1]
    second = []
    for d in range(1, rad_count):
        copy = pltpu.make_async_remote_copy(
            src_ref=mine,
            dst_ref=beside.at[d - 1],
            send_sem=send_b.at[d - 1],
            recv_sem=recv_b.at[d - 1],
            device_id={"rad": lax.rem(r + d, rad_count)},
            device_id_type=MESH,
        )
        copy.start()
        second.append(copy)
    total = mine[...]
    for d in range(1, rad_count):
        second[d - 1].wait_recv()
        total = total + beside[d - 1]
    whole[block_of(m), :] = total
    third = []
    for d in range(1, ma_count):
        copy = pltpu.make_async_remote_copy(
            src_ref=whole.at[block_of(m)],
            dst_ref=whole.at[block_of(m)],
            send_sem=send_c.at[d - 1],
            recv_sem=recv_c.at[d - 1],
            device_id={"ma": lax.rem(m + d, ma_count)},
            device_id_type=MESH,
        )
        copy.start()
        third.append(copy)
    sum_ref[...] = total
    for d in range(1, ma_count):
        sender = lax.rem(m + ma_count - d, ma_count)
        pltpu.make_async_remote_copy(
            src_ref=whole.at[block_of(sender)],
            dst_ref=whole.at[block_of(sender)],
            send_sem=send_c.at[d - 1],
            recv_sem=recv_c.at[d - 1],
            device_id={"ma": sender},
            device_id_type=MESH,
        ).wait_recv()
    for copy in first + second + third:
        copy.wait_send()
    value = whole[...]
    row = lax.broadcasted_iota(jnp.int32, (total_rows, 1), 0)
    radius = 0.35 + 0.65 * (row.astype(jnp.float32) + 0.5) / total_rows
    after = pltpu.roll(value, width - 1, 1)
    before = pltpu.roll(value, 1, 1)
    velocity_ref[0] = ((after - before) / (2.0 * radius)).astype(jnp.bfloat16)
    above = jnp.where(row == total_rows - 1, 0.0, pltpu.roll(value, total_rows - 1, 0))
    below = jnp.where(row == 0, 0.0, pltpu.roll(value, 1, 0))
    velocity_ref[1] = (-(above - below) * 0.5).astype(jnp.bfloat16)


def column_exchange(partial_value):
    rad_count = lax.axis_size("rad")
    ma_count = lax.axis_size("ma")
    total_rows, width = partial_value.shape
    rows = total_rows // ma_count
    dma = pltpu.SemaphoreType.DMA
    vmem = pl.BlockSpec(memory_space=pltpu.VMEM)
    summed, velocity = pl.pallas_call(
        functools.partial(column_kernel, rad_count, ma_count),
        out_shape=(
            jax.ShapeDtypeStruct((rows, width), jnp.float32),
            jax.ShapeDtypeStruct((2, total_rows, width), jnp.bfloat16),
        ),
        in_specs=[vmem],
        out_specs=(vmem, vmem),
        scratch_shapes=[
            pltpu.VMEM((ma_count - 1, rows, width), jnp.float32),
            pltpu.VMEM((rows, width), jnp.float32),
            pltpu.VMEM((rad_count - 1, rows, width), jnp.float32),
            pltpu.VMEM((total_rows, width), jnp.float32),
            dma((ma_count - 1,)),
            dma((ma_count - 1,)),
            dma((rad_count - 1,)),
            dma((rad_count - 1,)),
            dma((ma_count - 1,)),
            dma((ma_count - 1,)),
        ],
        compiler_params=pltpu.CompilerParams(collective_id=0, has_side_effects=True),
        name="column_exchange",
    )(partial_value)
    block = width // rad_count
    owned = lax.dynamic_slice_in_dim(summed, lax.axis_index("rad") * block, block, axis=1)
    return owned, velocity


def on_device(spectrum, radial_table, legendre, order_table, cylinder_row, column_weight):
    slot_count = spectrum.shape[1]
    degree_count = spectrum.shape[2]
    level_count = radial_table.shape[0]
    latitude_count = legendre.shape[2]
    rad_count = lax.axis_size("rad")
    ma_count = lax.axis_size("ma")
    total_rows = QROWS * ma_count
    my_orders = lax.dynamic_slice_in_dim(order_table, lax.axis_index("ma") * slot_count, slot_count)
    my_degrees = lax.axis_index("rad") * degree_count + jnp.arange(degree_count, dtype=jnp.int32)
    allowed = my_degrees[None, :] >= my_orders[:, None]
    tables = synthesis_tables(order_table)
    lat_rows = latitude_count // (rad_count * ma_count)
    if (
        latitude_count % (rad_count * LANES) == 0
        and degree_count % LANES == 0
        and slot_count % (GROUP * HALVES) == 0
        and slot_count // HALVES * level_count * 4 % LANES == 0
        and rad_count > 2
        and lat_rows % 16 == 0
    ):
        received = latitude_exchange(spectrum, radial_table, legendre, allowed, GROUP)
        groups = ma_count * HALVES
        coefficients = received.reshape(
            lat_rows, groups, level_count, 2, 2, slot_count // HALVES
        )
    else:
        masked_table = jnp.where(allowed[:, :, None], legendre, jnp.zeros_like(legendre))
        levels = jnp.einsum(
            "rn,ckln->rckl", radial_table, spectrum, preferred_element_type=jnp.float32
        ).astype(jnp.bfloat16)
        contribution = jnp.einsum(
            "klt,rckl->trck", masked_table, levels, preferred_element_type=jnp.float32
        )
        pieces = contribution.astype(jnp.bfloat16).reshape(
            rad_count, latitude_count // rad_count, level_count * 4 * slot_count
        )
        pieces = lax.all_to_all(pieces, "rad", split_axis=0, concat_axis=0, tiled=True)
        latitudes = jnp.sum(pieces.astype(jnp.float32), axis=0).astype(jnp.bfloat16)
        received = lax.all_to_all(latitudes, "ma", split_axis=0, concat_axis=1, tiled=True)
        coefficients = received.reshape(lat_rows, ma_count, level_count, 2, 2, slot_count)
        groups = ma_count
    tables = tables.reshape(2, groups, ma_count * slot_count // groups, 2 * NPHI)
    synthesis = jnp.einsum(
        "tsrfik,iskq->ftrq", coefficients, tables, preferred_element_type=jnp.float32
    ).astype(jnp.bfloat16)
    fields = synthesis[..., :NPHI].astype(jnp.float32)
    slope_field = synthesis[..., NPHI:].astype(jnp.float32)
    buoyancy = fields[0] - composition_weight * fields[1]
    weighted = (column_weight[:, :, None] * buoyancy).reshape(-1, NPHI)
    point_rows = cylinder_row.reshape(-1)
    row_ids = jnp.arange(total_rows, dtype=jnp.int32)
    selector = (row_ids[:, None] == point_rows[None, :]).astype(jnp.float32)
    partial_value = jnp.dot(
        selector, weighted, precision=lax.Precision.HIGHEST, preferred_element_type=jnp.float32
    )
    owned, velocity = column_exchange(partial_value)
    chooser = (point_rows[:, None] == row_ids[None, :]).astype(jnp.bfloat16)
    moved = jnp.einsum("pj,cjq->cpq", chooser, velocity, preferred_element_type=jnp.float32)
    moved = moved.reshape(2, lat_rows, level_count, NPHI)
    inverse = 1.0 / (0.35 + 0.65 * (cylinder_row.astype(jnp.float32) + 0.5) / total_rows)
    advected = fields - time_step * inverse[None, :, :, None] * (
        moved[1][None] * slope_field + moved[0][None] * fields
    )
    return (owned, advected)


def solution(mesh):
    return jax.shard_map(
        on_device,
        mesh=mesh,
        in_specs=(
            P(None, "ma", "rad", None),
            P(),
            P("ma", "rad", None),
            P(),
            P(("rad", "ma"), None),
            P(("rad", "ma"), None),
        ),
        out_specs=(P("ma", "rad"), P(None, ("rad", "ma"), None, None)),
        check_vma=False,
    )
```

```python
import functools
import math

import jax
import jax.numpy as jnp
from jax import lax
from jax.experimental import pallas as pl
from jax.experimental.pallas import tpu as pltpu
from jax.sharding import PartitionSpec as P

L = 512
NPHI = 1024
QROWS = 16
LANES = 128
GROUP = 8
HALVES = 1
MESH = pl.DeviceIdType.MESH


time_step = 0.05
composition_weight = 0.8


def synthesis_tables(order_table):
    def turn(steps):
        phase_index = order_table[:, None] * steps[None, :] % NPHI
        angles = phase_index.astype(jnp.float32) * (2.0 * math.pi / NPHI)
        return jnp.cos(angles), jnp.sin(angles)

    near_cos, near_sin = turn(jnp.arange(LANES, dtype=jnp.int32))
    far_cos, far_sin = turn(jnp.arange(NPHI // LANES, dtype=jnp.int32) * LANES)
    weights = jnp.where(order_table == 0, 1.0, 2.0).astype(jnp.float32) / math.sqrt(L)
    far_cos = far_cos * weights[:, None]
    far_sin = far_sin * weights[:, None]
    slopes = (order_table.astype(jnp.float32) / L)[:, None]
    return near_cos, near_sin, far_cos, far_sin, slopes


def plain_tables(pieces):
    count = pieces[0].shape[0]
    whole = pl.BlockSpec(memory_space=pltpu.VMEM)
    return pl.pallas_call(
        functools.partial(write_tables, slice(None)),
        out_shape=jax.ShapeDtypeStruct((2, count, 2 * NPHI), jnp.bfloat16),
        in_specs=[whole] * 5,
        out_specs=whole,
        name="tables",
    )(*pieces)


def write_tables(block, near_cos_ref, near_sin_ref, far_cos_ref, far_sin_ref, slope_ref, out_ref):
    near_cos = near_cos_ref[block, :]
    near_sin = near_sin_ref[block, :]
    slope = slope_ref[block, :]
    far_cos_all = far_cos_ref[block, :]
    far_sin_all = far_sin_ref[block, :]
    for a in range(far_cos_ref.shape[1]):
        far_cos = far_cos_all[:, a : a + 1]
        far_sin = far_sin_all[:, a : a + 1]
        cosine = far_cos * near_cos - far_sin * near_sin
        sine = far_sin * near_cos + far_cos * near_sin
        value = slice(a * LANES, (a + 1) * LANES)
        turned = slice(NPHI + a * LANES, NPHI + (a + 1) * LANES)
        out_ref[0, block, value] = cosine.astype(jnp.bfloat16)
        out_ref[1, block, value] = (-sine).astype(jnp.bfloat16)
        out_ref[0, block, turned] = (-sine * slope).astype(jnp.bfloat16)
        out_ref[1, block, turned] = (-cosine * slope).astype(jnp.bfloat16)


def latitude_kernel(rad_count, ma_count, chunks, mask_ref, radial_ref, near_cos_ref, near_sin_ref,
                    far_cos_ref, far_sin_ref, slope_ref, spectrum_ref, legendre_ref, out_ref, table_ref,
                    spectrum_buf, legendre_buf, own, out_up, out_down, in_up, in_down, finished, ready, arrived,
                    fetch_sem, up_send, up_recv, down_send, down_recv, ma_send, ma_recv):
    r = lax.axis_index("rad")
    m = lax.axis_index("ma")
    last = rad_count - 1
    _, _, slots, degrees, modes = spectrum_buf.shape
    rows = radial_ref.shape[1]
    lanes = own.shape[3]
    share = out_ref.shape[0]

    def fetch(c, slot):
        piece = pl.ds(c * slots, slots)
        return (
            pltpu.make_async_copy(
                spectrum_ref.at[:, piece], spectrum_buf.at[slot], fetch_sem.at[0, slot]
            ),
            pltpu.make_async_copy(
                legendre_ref.at[piece], legendre_buf.at[slot], fetch_sem.at[1, slot]
            ),
        )

    for copy in fetch(0, 0):
        copy.start()

    barrier = pltpu.get_barrier_semaphore()
    for d in range(1, ma_count):
        pl.semaphore_signal(
            barrier, inc=1, device_id={"ma": lax.rem(m + d, ma_count)}, device_id_type=MESH
        )
    for d in range(1, rad_count):
        pl.semaphore_signal(
            barrier, inc=1, device_id={"rad": lax.rem(r + d, rad_count)}, device_id_type=MESH
        )
    pl.semaphore_wait(barrier, ma_count + rad_count - 2)

    def up(c, target):
        return pltpu.make_async_remote_copy(
            src_ref=out_up.at[c, target],
            dst_ref=in_up.at[c, target],
            send_sem=up_send.at[c, target],
            recv_sem=up_recv.at[c, target],
            device_id={"rad": lax.rem(r + 1, rad_count)},
            device_id_type=MESH,
        )

    def down(c, target):
        return pltpu.make_async_remote_copy(
            src_ref=out_down.at[c, target],
            dst_ref=in_down.at[c, target],
            send_sem=down_send.at[c, target],
            recv_sem=down_recv.at[c, target],
            device_id={"rad": lax.rem(r + last, rad_count)},
            device_id_type=MESH,
        )

    half_chunks = chunks // HALVES
    kept_slots = half_chunks * slots
    width = rows * kept_slots

    def landing(source, h):
        start = (source * HALVES + h) * width
        return arrived.at[:, pl.ds(pl.multiple_of(start, width), width)]

    def hand_over(h, d):
        peer = lax.rem(m + d, ma_count)
        return pltpu.make_async_remote_copy(
            src_ref=ready.at[h, pl.ds(pl.multiple_of(peer * share, share), share)],
            dst_ref=landing(m, h),
            send_sem=ma_send.at[h, d - 1],
            recv_sem=ma_recv.at[h, d - 1],
            device_id={"ma": peer},
            device_id_type=MESH,
        )

    def compute(c, carry):
        slot = lax.rem(c, 2)

        @pl.when(c + 1 < chunks)
        def _():
            for copy in fetch(c + 1, 1 - slot):
                copy.start()

        for copy in fetch(c, slot):
            copy.wait()
        levels = jnp.zeros((rows, slots * degrees), jnp.float32)
        for part in range(spectrum_buf.shape[1]):
            levels += lax.dot_general(
                radial_ref[part],
                spectrum_buf[slot, part].reshape(slots * degrees, modes),
                (((1,), (1,)), ((), ())),
                preferred_element_type=jnp.float32,
            )
        for s in range(slots):
            kept = levels[:, s * degrees : (s + 1) * degrees] * mask_ref[c * slots + s]
            sums = jnp.dot(
                kept.astype(jnp.bfloat16), legendre_buf[slot, s], preferred_element_type=jnp.float32
            )
            for target in range(rad_count):
                own[c, target, s * rows : (s + 1) * rows, :] = sums[
                    :, target * lanes : (target + 1) * lanes
                ]

        @pl.when(r == 0)
        def _():
            for target in range(last, 0, -1):
                out_up[c, target] = own[c, target].astype(jnp.bfloat16)
                up(c, target).start()

        @pl.when(r == last)
        def _():
            for target in range(last):
                out_down[c, target] = own[c, target].astype(jnp.bfloat16)
                down(c, target).start()

        return carry

    lax.fori_loop(0, chunks, compute, 0)

    def relay_up(step, here):
        c = step - (r - 1)
        for target in range(last, 0, -1):

            @pl.when(here & (r > 0) & (r < target) & (c >= 0) & (c < chunks))
            def _():
                up(c, target).wait_recv()
                out_up[c, target] = (
                    own[c, target] + in_up[c, target].astype(jnp.float32)
                ).astype(jnp.bfloat16)
                up(c, target).start()

    def relay_down(step, here):
        c = step - (last - r - 1)
        for target in range(last):

            @pl.when(here & (r < last) & (r > target) & (c >= 0) & (c < chunks))
            def _():
                down(c, target).wait_recv()
                out_down[c, target] = (
                    own[c, target] + in_down[c, target].astype(jnp.float32)
                ).astype(jnp.bfloat16)
                down(c, target).start()

    def finish(c):
        @pl.when(r > 0)
        def _():
            up(c, r).wait_recv()
            own[c, r] += in_up[c, r].astype(jnp.float32)

        @pl.when(r < last)
        def _():
            down(c, r).wait_recv()
            own[c, r] += in_down[c, r].astype(jnp.float32)

        first = lax.rem(c, half_chunks) * slots
        for s in range(slots):
            finished[pl.ds(first + s, rows, stride=kept_slots), :] = own[
                c, r, s * rows : (s + 1) * rows, :
            ]

        @pl.when(lax.rem(c, half_chunks) == half_chunks - 1)
        def _():
            h = c // half_chunks
            ready[h] = finished[...].T.astype(jnp.bfloat16)
            for d in range(1, ma_count):
                hand_over(h, d).start()
            place = pl.ds(pl.multiple_of((m * HALVES + h) * width, width), width)
            arrived[:, place] = ready[h, pl.ds(pl.multiple_of(m * share, share), share), :]

    nearer_top = 2 * r > last
    nearer_bottom = 2 * r <= last

    table_block = table_ref.shape[1] // chunks

    def pass_on(step, carry):
        relay_up(step, nearer_top)
        relay_down(step, nearer_bottom)
        relay_up(step, nearer_bottom)
        relay_down(step, nearer_top)

        @pl.when(step >= last - 1)
        def _():
            finish(step - (last - 1))

        @pl.when(step < chunks)
        def _():
            write_tables(
                pl.ds(pl.multiple_of(step * table_block, table_block), table_block),
                near_cos_ref, near_sin_ref, far_cos_ref, far_sin_ref, slope_ref, table_ref,
            )

        return carry

    lax.fori_loop(0, chunks + last - 1, pass_on, 0)

    for h in range(HALVES):
        for d in range(1, ma_count):
            sender = lax.rem(m + ma_count - d, ma_count)
            pltpu.make_async_remote_copy(
                src_ref=ready.at[h, pl.ds(0, share)],
                dst_ref=landing(sender, h),
                send_sem=ma_send.at[h, d - 1],
                recv_sem=ma_recv.at[h, d - 1],
                device_id={"ma": sender},
                device_id_type=MESH,
            ).wait_recv()
            hand_over(h, d).wait_send()

    def drain(c, carry):
        for target in range(rad_count):

            @pl.when(r < target)
            def _():
                up(c, target).wait_send()

            @pl.when(r > target)
            def _():
                down(c, target).wait_send()

        return carry

    lax.fori_loop(0, chunks, drain, 0)
    out_ref[...] = arrived[...]


def latitude_exchange(spectrum, radial_table, legendre, allowed, pieces, slots):
    rad_count = lax.axis_size("rad")
    ma_count = lax.axis_size("ma")
    parts, slot_count, degrees, modes = spectrum.shape
    level_count = radial_table.shape[0]
    latitude_count = legendre.shape[2]
    rows = level_count * parts
    chunks = slot_count // slots
    lanes = latitude_count // rad_count
    share = lanes // ma_count
    spread = jnp.einsum("rn,cd->crdn", radial_table, jnp.eye(parts, dtype=radial_table.dtype))
    spread = spread.reshape(parts, rows, modes)
    dma = pltpu.SemaphoreType.DMA
    vmem = pl.BlockSpec(memory_space=pltpu.VMEM)
    hbm = pl.BlockSpec(memory_space=pl.ANY)
    travelling = pltpu.VMEM((chunks, rad_count, slots * rows, lanes), jnp.bfloat16)
    return pl.pallas_call(
        functools.partial(latitude_kernel, rad_count, ma_count, chunks),
        out_shape=(
            jax.ShapeDtypeStruct((share, ma_count * rows * slot_count), jnp.bfloat16),
            jax.ShapeDtypeStruct((2, ma_count * slot_count, 2 * NPHI), jnp.bfloat16),
        ),
        in_specs=[vmem] * 7 + [hbm, hbm],
        out_specs=(vmem, vmem),
        scratch_shapes=[
            pltpu.VMEM((2, parts, slots, degrees, modes), jnp.bfloat16),
            pltpu.VMEM((2, slots, degrees, latitude_count), jnp.bfloat16),
            pltpu.VMEM((chunks, rad_count, slots * rows, lanes), jnp.float32),
            travelling,
            travelling,
            travelling,
            travelling,
            pltpu.VMEM((rows * slot_count // HALVES, lanes), jnp.float32),
            pltpu.VMEM((HALVES, lanes, rows * slot_count // HALVES), jnp.bfloat16),
            pltpu.VMEM((share, ma_count * rows * slot_count), jnp.bfloat16),
            dma((2, 2)),
            dma((chunks, rad_count)),
            dma((chunks, rad_count)),
            dma((chunks, rad_count)),
            dma((chunks, rad_count)),
            dma((HALVES, ma_count - 1)),
            dma((HALVES, ma_count - 1)),
        ],
        compiler_params=pltpu.CompilerParams(
            collective_id=1, has_side_effects=True, vmem_limit_bytes=56 * 1024 * 1024
        ),
        name="latitude_exchange",
    )(allowed.astype(jnp.float32)[:, None, :], spread, *pieces, spectrum, legendre)


def column_kernel(rad_count, ma_count, partial_ref, sum_ref, velocity_ref, arrived, mine, beside, whole,
                  send_a, recv_a, send_b, recv_b, send_c, recv_c):
    r = lax.axis_index("rad")
    m = lax.axis_index("ma")
    total_rows, width = partial_ref.shape
    rows = total_rows // ma_count
    barrier = pltpu.get_barrier_semaphore()
    for d in range(1, ma_count):
        pl.semaphore_signal(
            barrier, inc=1, device_id={"ma": lax.rem(m + d, ma_count)}, device_id_type=MESH
        )
    for d in range(1, rad_count):
        pl.semaphore_signal(
            barrier, inc=1, device_id={"rad": lax.rem(r + d, rad_count)}, device_id_type=MESH
        )
    pl.semaphore_wait(barrier, ma_count + rad_count - 2)

    def block_of(index):
        return pl.ds(pl.multiple_of(index * rows, rows), rows)

    first = []
    for d in range(1, ma_count):
        peer = lax.rem(m + d, ma_count)
        copy = pltpu.make_async_remote_copy(
            src_ref=partial_ref.at[block_of(peer)],
            dst_ref=arrived.at[d - 1],
            send_sem=send_a.at[d - 1],
            recv_sem=recv_a.at[d - 1],
            device_id={"ma": peer},
            device_id_type=MESH,
        )
        copy.start()
        first.append(copy)
    mine[...] = partial_ref[block_of(m), :]
    for d in range(1, ma_count):
        first[d - 1].wait_recv()
        mine[...] += arrived[d - 1]
    second = []
    for d in range(1, rad_count):
        copy = pltpu.make_async_remote_copy(
            src_ref=mine,
            dst_ref=beside.at[d - 1],
            send_sem=send_b.at[d - 1],
            recv_sem=recv_b.at[d - 1],
            device_id={"rad": lax.rem(r + d, rad_count)},
            device_id_type=MESH,
        )
        copy.start()
        second.append(copy)
    total = mine[...]
    for d in range(1, rad_count):
        second[d - 1].wait_recv()
        total = total + beside[d - 1]
    whole[block_of(m), :] = total
    third = []
    for d in range(1, ma_count):
        copy = pltpu.make_async_remote_copy(
            src_ref=whole.at[block_of(m)],
            dst_ref=whole.at[block_of(m)],
            send_sem=send_c.at[d - 1],
            recv_sem=recv_c.at[d - 1],
            device_id={"ma": lax.rem(m + d, ma_count)},
            device_id_type=MESH,
        )
        copy.start()
        third.append(copy)
    sum_ref[...] = total
    for d in range(1, ma_count):
        sender = lax.rem(m + ma_count - d, ma_count)
        pltpu.make_async_remote_copy(
            src_ref=whole.at[block_of(sender)],
            dst_ref=whole.at[block_of(sender)],
            send_sem=send_c.at[d - 1],
            recv_sem=recv_c.at[d - 1],
            device_id={"ma": sender},
            device_id_type=MESH,
        ).wait_recv()
    for copy in first + second + third:
        copy.wait_send()
    value = whole[...]
    row = lax.broadcasted_iota(jnp.int32, (total_rows, 1), 0)
    radius = 0.35 + 0.65 * (row.astype(jnp.float32) + 0.5) / total_rows
    after = pltpu.roll(value, width - 1, 1)
    before = pltpu.roll(value, 1, 1)
    velocity_ref[0] = ((after - before) / (2.0 * radius)).astype(jnp.bfloat16)
    above = jnp.where(row == total_rows - 1, 0.0, pltpu.roll(value, total_rows - 1, 0))
    below = jnp.where(row == 0, 0.0, pltpu.roll(value, 1, 0))
    velocity_ref[1] = (-(above - below) * 0.5).astype(jnp.bfloat16)


def column_exchange(partial_value):
    rad_count = lax.axis_size("rad")
    ma_count = lax.axis_size("ma")
    total_rows, width = partial_value.shape
    rows = total_rows // ma_count
    dma = pltpu.SemaphoreType.DMA
    vmem = pl.BlockSpec(memory_space=pltpu.VMEM)
    summed, velocity = pl.pallas_call(
        functools.partial(column_kernel, rad_count, ma_count),
        out_shape=(
            jax.ShapeDtypeStruct((rows, width), jnp.float32),
            jax.ShapeDtypeStruct((2, total_rows, width), jnp.bfloat16),
        ),
        in_specs=[vmem],
        out_specs=(vmem, vmem),
        scratch_shapes=[
            pltpu.VMEM((ma_count - 1, rows, width), jnp.float32),
            pltpu.VMEM((rows, width), jnp.float32),
            pltpu.VMEM((rad_count - 1, rows, width), jnp.float32),
            pltpu.VMEM((total_rows, width), jnp.float32),
            dma((ma_count - 1,)),
            dma((ma_count - 1,)),
            dma((rad_count - 1,)),
            dma((rad_count - 1,)),
            dma((ma_count - 1,)),
            dma((ma_count - 1,)),
        ],
        compiler_params=pltpu.CompilerParams(collective_id=0, has_side_effects=True),
        name="column_exchange",
    )(partial_value)
    block = width // rad_count
    owned = lax.dynamic_slice_in_dim(summed, lax.axis_index("rad") * block, block, axis=1)
    return owned, velocity


def on_device(spectrum, radial_table, legendre, order_table, cylinder_row, column_weight):
    slot_count = spectrum.shape[1]
    degree_count = spectrum.shape[2]
    level_count = radial_table.shape[0]
    latitude_count = legendre.shape[2]
    rad_count = lax.axis_size("rad")
    ma_count = lax.axis_size("ma")
    total_rows = QROWS * ma_count
    my_orders = lax.dynamic_slice_in_dim(order_table, lax.axis_index("ma") * slot_count, slot_count)
    my_degrees = lax.axis_index("rad") * degree_count + jnp.arange(degree_count, dtype=jnp.int32)
    allowed = my_degrees[None, :] >= my_orders[:, None]
    pieces = synthesis_tables(order_table)
    lat_rows = latitude_count // (rad_count * ma_count)
    if (
        latitude_count % (rad_count * LANES) == 0
        and degree_count % LANES == 0
        and slot_count % (GROUP * HALVES) == 0
        and slot_count // HALVES * level_count * 4 % LANES == 0
        and rad_count > 2
        and lat_rows % 16 == 0
    ):
        received, tables = latitude_exchange(
            spectrum, radial_table, legendre, allowed, pieces, GROUP
        )
        groups = ma_count * HALVES
        coefficients = received.reshape(
            lat_rows, groups, level_count, 2, 2, slot_count // HALVES
        )
    else:
        tables = plain_tables(pieces)
        masked_table = jnp.where(allowed[:, :, None], legendre, jnp.zeros_like(legendre))
        levels = jnp.einsum(
            "rn,ckln->rckl", radial_table, spectrum, preferred_element_type=jnp.float32
        ).astype(jnp.bfloat16)
        contribution = jnp.einsum(
            "klt,rckl->trck", masked_table, levels, preferred_element_type=jnp.float32
        )
        sums = contribution.astype(jnp.bfloat16).reshape(
            rad_count, latitude_count // rad_count, level_count * 4 * slot_count
        )
        sums = lax.all_to_all(sums, "rad", split_axis=0, concat_axis=0, tiled=True)
        latitudes = jnp.sum(sums.astype(jnp.float32), axis=0).astype(jnp.bfloat16)
        received = lax.all_to_all(latitudes, "ma", split_axis=0, concat_axis=1, tiled=True)
        coefficients = received.reshape(lat_rows, ma_count, level_count, 2, 2, slot_count)
        groups = ma_count
    tables = tables.reshape(2, groups, ma_count * slot_count // groups, 2 * NPHI)
    synthesis = jnp.einsum(
        "tsrfik,iskq->ftrq", coefficients, tables, preferred_element_type=jnp.float32
    ).astype(jnp.bfloat16)
    fields = synthesis[..., :NPHI].astype(jnp.float32)
    slope_field = synthesis[..., NPHI:].astype(jnp.float32)
    buoyancy = fields[0] - composition_weight * fields[1]
    weighted = (column_weight[:, :, None] * buoyancy).reshape(-1, NPHI)
    point_rows = cylinder_row.reshape(-1)
    row_ids = jnp.arange(total_rows, dtype=jnp.int32)
    selector = (row_ids[:, None] == point_rows[None, :]).astype(jnp.float32)
    partial_value = jnp.dot(
        selector, weighted, precision=lax.Precision.HIGHEST, preferred_element_type=jnp.float32
    )
    owned, velocity = column_exchange(partial_value)
    chooser = (point_rows[:, None] == row_ids[None, :]).astype(jnp.bfloat16)
    moved = jnp.einsum("pj,cjq->cpq", chooser, velocity, preferred_element_type=jnp.float32)
    moved = moved.reshape(2, lat_rows, level_count, NPHI)
    inverse = 1.0 / (0.35 + 0.65 * (cylinder_row.astype(jnp.float32) + 0.5) / total_rows)
    advected = fields - time_step * inverse[None, :, :, None] * (
        moved[1][None] * slope_field + moved[0][None] * fields
    )
    return (owned, advected)


def solution(mesh):
    return jax.shard_map(
        on_device,
        mesh=mesh,
        in_specs=(
            P(None, "ma", "rad", None),
            P(),
            P("ma", "rad", None),
            P(),
            P(("rad", "ma"), None),
            P(("rad", "ma"), None),
        ),
        out_specs=(P("ma", "rad"), P(None, ("rad", "ma"), None, None)),
        check_vma=False,
    )
```
